128 devices in a mesh: row: 16 (over x, z), col: 8 (over y, core).
Axes of the slice: x: 4, y: 4, z: 4, core: 2. Of those that a mesh axis runs over, the one named last changes fastest.
Arguments:
- psi: bfloat16 [16, 16, 3, 256, 256], P('row', None, None, 'col'), may hold values from -6 to 6
- left_ops: bfloat16 [16, 16, 32, 256, 256], P('row', None, 'col'), may hold values from -0.375 to 0.375
- right_ops: bfloat16 [16, 16, 32, 256, 256], P('row', None, 'col'), may hold values from -0.0625 to 0.0625
- mpo_pattern: int32 [16, 16, 32], P('row', None, 'col'), may hold values 0 or 1
- block_sizes: int32 [2, 16, 16], P(None, 'row'), may hold values from 1 to 256, 2560 in all within a row
Outputs:
- h_psi: bfloat16 [16, 16, 3, 256, 256], P('row', None, None, 'col')
The draws below stay inside these ranges and needn't reach their ends.
Inputs may be any that keep to these rules, and one draw needn't show every extreme that they name: `block_sizes`: for each index and sector a, the 16 sizes along the last dimension sum to 2560.
All inputs are finite; a program needn't handle non-finite values. No bound on the sum of `mpo_pattern` on one device may be relied on, other than what follows from the above.
Results may differ from the reference program's by a relative error of at most 0.005.
Values may be sent and summed in bfloat16 or wider, within the bound.
No kernel may reach another device: no remote copies, remote signals or barrier semaphores. Data moves between devices by JAX's collectives and lax.ppermute only.
A program may use at most 128 MiB of HBM per device.

```python
import math
import jax
import jax.numpy as jnp
import numpy as np
from jax import lax

BLK = 256
W = 32
NVEC = 3
NA = 16
NB = 16


def place_ends(result, rng, smallest, high):
    longest = result.shape.index(max(result.shape))
    spots = []
    for shift in (0, 1):
        where = [jax.random.randint(jax.random.fold_in(rng, axis), (), 0, length) for axis, length in enumerate(result.shape)]
        where[longest] = (where[longest] + shift) % result.shape[longest]
        spots.append(tuple(where))
    return result.at[spots[0]].set(smallest).at[spots[1]].set(high)


def level_of(key, extent, cuts, low, high):
    loudness = 1.0
    for axis_at, blocks in cuts:
        steps = jax.random.uniform(jax.random.fold_in(jax.random.fold_in(key, 6), axis_at), (blocks,), jnp.float32, low / len(cuts), high / len(cuts))
        loudness = loudness * jnp.repeat(jnp.exp(steps), extent[axis_at] // blocks).reshape((-1,) + (1,) * (len(extent) - 1 - axis_at))
    return loudness


def profile(number_of, total, most, skew):
    portions = [(1 << 20) // math.isqrt(grade ** skew) + 1 for grade in range(2, number_of + 1)]
    spare, holding = total - most - (number_of - 1), [1] * (number_of - 1)
    while spare > 0:
        candidates = [i for i in range(number_of - 1) if holding[i] < most]
        pool, budget = sum([portions[i] for i in candidates]), spare
        for i in candidates:
            addition = min(most - holding[i], max(1, budget * portions[i] // pool), spare)
            holding[i] = holding[i] + addition
            spare = spare - addition
    return np.array([most] + holding)


def ragged_sizes(stream_key, number_of, total, limit, slope):
    if number_of == 2:
        one = jax.random.randint(stream_key, (), max(1, total - limit), min(limit, total - 1) + 1)
        return jnp.stack([one, total - one])
    tallies = jnp.asarray(profile(number_of, total, limit, slope), jnp.int32)
    couples = (number_of - 1) // 2
    source_of, sink = tallies[1:1 + 2 * couples:2], tallies[2:2 + 2 * couples:2]
    room = jnp.minimum(source_of - 1, limit - sink)
    shifted = jax.random.randint(jax.random.fold_in(stream_key, 1), (couples,), 0, 1 << 20) % (room + 1)
    tallies = tallies.at[1:1 + 2 * couples:2].set(source_of - shifted).at[2:2 + 2 * couples:2].set(sink + shifted)
    return tallies[jax.random.permutation(jax.random.fold_in(stream_key, 2), number_of)]


def centred(rng, extent, deviation, reach, pieces=(), held_as=jnp.bfloat16):
    array = jax.random.normal(rng, extent, jnp.float32) * deviation
    if len(pieces) > 0:
        array = level_of(rng, extent, pieces, -0.22, 0.18) * array
    return jnp.clip(array, min=-reach, max=reach).astype(held_as)


def setup_inputs(seed: int = 0) -> dict:
    key_of = jax.random.split(jax.random.key(seed), 6)
    return {
        "psi": centred(key_of[0], (NA, NB, NVEC, BLK, BLK), 1.0, 6.0, ((0, 16), (3, 8))),
        "left_ops": centred(key_of[1], (NA, NB, W, BLK, BLK), BLK ** -0.5, 0.375, ((0, 16), (2, 8))),
        "right_ops": centred(key_of[2], (NB, NA, W, BLK, BLK), (BLK * W) ** -0.5, 0.0625, ((0, 16), (2, 8))),
        "mpo_pattern": place_ends((jax.random.randint(key_of[3], (NA, NB, W), 0, 4) < 3).astype(jnp.int32), jax.random.fold_in(key_of[3], 1), 0, 1),
        "block_sizes": jax.vmap(lambda own: ragged_sizes(own, NB, NB * BLK * 5 // 8, BLK, 2))(jax.random.split(key_of[4], 2 * NA)).reshape((2, NA, NB)).astype(jnp.int32),
    }


def reference(psi, left_ops, right_ops, mpo_pattern, block_sizes):
    index = jnp.arange(BLK, dtype=jnp.int32)

    def one_sector(sector):
        live_rows = index[None, :] < block_sizes[0, sector][:, None]
        live_cols = index[None, :] < block_sizes[1, sector][:, None]
        keep = live_rows[:, None, :, None] & live_cols[:, None, None, :]
        live = jnp.where(keep, psi[sector], jnp.zeros((), jnp.bfloat16)).astype(jnp.bfloat16)
        terms = jnp.einsum("bkrm,bvmc->bkvrc", left_ops[sector].astype(jnp.float32), live.astype(jnp.float32))
        terms = (terms * mpo_pattern[sector][:, :, None, None, None].astype(jnp.float32)).astype(jnp.bfloat16)
        right = right_ops[:, sector]
        total = jnp.einsum("bkvrm,bkcm->bvrc", terms.astype(jnp.float32), right.astype(jnp.float32))
        return jnp.where(keep, total, jnp.zeros((), jnp.float32)).astype(jnp.bfloat16)

    return lax.map(one_sector, jnp.arange(NA, dtype=jnp.int32))
```

```python
import functools

import jax
import jax.numpy as jnp
from jax import lax
from jax.experimental import pallas as pl
from jax.experimental.pallas import tpu as pltpu
from jax.sharding import PartitionSpec as P


SIDE = 4
CORES = 2
GROUPS = (
    ((0, 0), (1, 0), (3, 0), (0, 1), (0, 3), (1, 1)),
    ((3, 3), (1, 3), (3, 1), (2, 0), (0, 2)),
    ((2, 1), (2, 3), (1, 2)),
    ((3, 2), (2, 2)),
)
CUTS = (5, 10)


def row_shift(dx, dz):
    return [
        (x * SIDE + z, (x + dx) % SIDE * SIDE + (z + dz) % SIDE)
        for x in range(SIDE)
        for z in range(SIDE)
    ]


def col_shift(dy, dc):
    return [
        (y * CORES + c, (y + dy) % SIDE * CORES + (c + dc) % CORES)
        for y in range(SIDE)
        for c in range(CORES)
    ]


def pair_kernel(first, count, where, sizes, pattern, left, *refs):
    rights, psis = refs[:count], refs[count : count + SIDE * CORES]
    keep, give, left_v, right_v, live, terms, total, sems = refs[count + SIDE * CORES :]
    y, core = where[0], where[1]

    def right_copy(i, k, source):
        columns = pl.ds(k * 256, 256)
        return pltpu.make_async_copy(source.at[k], right_v.at[i, :, columns], sems.at[i, k])

    def left_copy(i):
        return pltpu.make_async_copy(left.at[where[2 + first + i]], left_v.at[i], sems.at[i, 4])

    def psi_copy(i, n):
        dy, dc = n // CORES, n % CORES
        start = pl.multiple_of(
            lax.rem(y + SIDE - dy, SIDE) * 64 + lax.rem(core + dc, CORES) * 32, 32
        )
        return pltpu.make_async_copy(
            psis[n].at[where[2 + first + i]], live.at[i, :, pl.ds(start, 32), :], sems.at[i, 5 + n]
        )

    for i in range(count):
        for n in range(SIDE * CORES):
            psi_copy(i, n).start()
        left_copy(i).start()
        for k in range(4):
            right_copy(i, k, rights[i]).start()

    def one_pair(i, carry):
        pair = where[2 + first + i]
        rows, columns = sizes[0, pair], sizes[1, pair]
        for n in range(SIDE * CORES):
            psi_copy(i, n).wait()
        left_copy(i).wait()
        row_at = lax.broadcasted_iota(jnp.int32, (256, 256), 0)
        column_at = lax.broadcasted_iota(jnp.int32, (256, 256), 1)
        inside = (row_at < rows) & (column_at < columns)
        for v in range(3):
            masked = jnp.where(inside, live[i, v].astype(jnp.float32), 0.0).astype(jnp.bfloat16)
            for k in range(4):
                term = jnp.dot(left_v[i, k], masked, preferred_element_type=jnp.float32)
                term = term * pattern[pair, k].astype(jnp.float32)
                terms[v * 256 : v * 256 + 256, k * 256 : k * 256 + 256] = term.astype(jnp.bfloat16)
        for k in range(4):
            right_copy(i, k, rights[0]).wait()
        for v in range(3):
            summed = lax.dot_general(
                terms[v * 256 : v * 256 + 256, :],
                right_v[i],
                (((1,), (1,)), ((), ())),
                preferred_element_type=jnp.float32,
            )
            total[v] = jnp.where(inside, summed, 0.0)
        for dy in range(SIDE):
            base = lax.rem(y + dy, SIDE) * 64
            mine = pl.multiple_of(base + core * 32, 32)
            other = pl.multiple_of(base + (1 - core) * 32, 32)
            for v in range(3):
                keep[dy, i, v] = total[v, pl.ds(mine, 32), :]
                give[dy, i, v] = total[v, pl.ds(other, 32), :].astype(jnp.bfloat16)
        return carry

    lax.fori_loop(0, count, one_pair, 0)


def pair_sums(first, where, sizes, pattern, left, rights, psis):
    count = len(rights)
    anywhere = pl.BlockSpec(memory_space=pl.ANY)
    vmem = pl.BlockSpec(memory_space=pltpu.VMEM)
    return pl.pallas_call(
        functools.partial(pair_kernel, first, count),
        grid_spec=pltpu.PrefetchScalarGridSpec(
            num_scalar_prefetch=3,
            in_specs=[anywhere] * (1 + count + len(psis)),
            out_specs=[vmem, vmem],
            scratch_shapes=[
                pltpu.VMEM((count, 4, 256, 256), jnp.bfloat16),
                pltpu.VMEM((count, 256, 1024), jnp.bfloat16),
                pltpu.VMEM((count, 3, 256, 256), jnp.bfloat16),
                pltpu.VMEM((768, 1024), jnp.bfloat16),
                pltpu.VMEM((3, 256, 256), jnp.float32),
                pltpu.SemaphoreType.DMA((count, 13)),
            ],
        ),
        out_shape=[
            jax.ShapeDtypeStruct((SIDE, count, 3, 32, 256), jnp.float32),
            jax.ShapeDtypeStruct((SIDE, count, 3, 32, 256), jnp.bfloat16),
        ],
        cost_estimate=pl.CostEstimate(
            flops=count * 805306368, bytes_accessed=count * 2000000, transcendentals=0
        ),
        name="pair_sums",
    )(where, sizes, pattern, left, *rights, *psis)


def place_kernel(first, parts, where, *refs):
    operands, result, out, sems = refs[: 4 * parts], refs[-3], refs[-2], refs[-1]
    copies = []
    at = 0
    for p in range(parts):
        own, one, two, three = operands[4 * p : 4 * p + 4]
        size = own.shape[0]
        out[at : at + size] = (
            own[...]
            + one[...].astype(jnp.float32)
            + two[...].astype(jnp.float32)
            + three[...].astype(jnp.float32)
        ).astype(jnp.bfloat16)
        for i in range(at, at + size):
            copy = pltpu.make_async_copy(out.at[i], result.at[where[2 + first + i]], sems.at[i])
            copy.start()
            copies.append(copy)
        at += size
    for copy in copies:
        copy.wait()


def place(first, where, parts, result):
    count = sum(part[0].shape[0] for part in parts)
    operands = [array for part in parts for array in part]
    vmem = pl.BlockSpec(memory_space=pltpu.VMEM)
    in_specs = [vmem] * len(operands)
    aliases = {}
    if result is not None:
        aliases = {1 + len(operands): 0}
        operands.append(result)
        in_specs.append(pl.BlockSpec(memory_space=pl.ANY))
    return pl.pallas_call(
        functools.partial(place_kernel, first, len(parts)),
        grid_spec=pltpu.PrefetchScalarGridSpec(
            num_scalar_prefetch=1,
            in_specs=in_specs,
            out_specs=pl.BlockSpec(memory_space=pl.ANY),
            scratch_shapes=[
                pltpu.VMEM((count, 3, 32, 256), jnp.bfloat16),
                pltpu.SemaphoreType.DMA((count,)),
            ],
        ),
        out_shape=jax.ShapeDtypeStruct((16, 3, 32, 256), jnp.bfloat16),
        input_output_aliases=aliases,
        compiler_params=pltpu.CompilerParams(vmem_limit_bytes=16 << 20),
        cost_estimate=pl.CostEstimate(
            flops=count * 100000, bytes_accessed=count * 300000, transcendentals=0
        ),
        name="place",
    )(where, *operands)


def tied(value, other):
    return lax.optimization_barrier((value, other))[0]


def shards(psi, left_ops, right_ops, mpo_pattern, block_sizes):
    row, col = lax.axis_index("row"), lax.axis_index("col")
    x, z, y, core = row >> 2, row & 3, col >> 1, col & 1
    right, left = right_ops[0], left_ops[0]
    sizes, pattern = block_sizes[:, 0], mpo_pattern[0]
    shifts = [shift for group in GROUPS for shift in group]
    sources = [(x - dx & 3) * SIDE + (z - dz & 3) for dx, dz in shifts]
    where = jnp.stack([y, core, *sources]).astype(jnp.int32)

    rights = []
    for n, (dx, dz) in enumerate(shifts):
        if n in CUTS:
            right = tied(right, rights[-1][0])
        block = lax.dynamic_index_in_dim(
            right, (x + dx & 3) * SIDE + (z + dz & 3), 0, keepdims=False
        )
        rights.append((block, dx, dz))
    moved = []
    for block, dx, dz in rights:
        if (dx, dz) != (0, 0):
            block = lax.ppermute(block, "row", row_shift(dx, dz))
        moved.append(block)

    psis = []
    for dy in range(SIDE):
        mine = psi[0]
        if dy:
            mine = lax.ppermute(mine, "col", col_shift(dy, 0))
        psis += [mine, lax.ppermute(mine, "col", col_shift(0, 1))]

    parts = []
    first = 0
    for group in GROUPS:
        keep, give = pair_sums(
            first, where, sizes, pattern, left, moved[first : first + len(group)], psis
        )
        given = lax.ppermute(give, "col", col_shift(0, 1))
        summed = [keep[dy] + given[dy].astype(jnp.float32) for dy in range(SIDE)]
        sent = [summed[dy].astype(jnp.bfloat16) for dy in range(SIDE)]
        arrived = []
        for dy in range(1, SIDE):
            arrived.append(lax.ppermute(sent[dy], "col", col_shift(dy, 0)))
        parts.append([summed[0], *arrived])
        first += len(group)
    result = place(0, where, parts[:-1], None)
    result = place(first - len(GROUPS[-1]), where, parts[-1:], result)
    return result[None]


def solution(mesh):
    in_specs = (
        P("row", None, None, "col", None),
        P("row", None, "col", None, None),
        P("row", None, "col", None, None),
        P("row", None, "col"),
        P(None, "row", None),
    )
    out_specs = P("row", None, None, "col", None)

    return jax.shard_map(shards, mesh=mesh, in_specs=in_specs, out_specs=out_specs, check_vma=False)
```
